32 devices in a mesh: col: 8 (over z, x), row: 4 (over y, core).
Axes of the slice: x: 2, y: 2, z: 4, core: 2. Of those that a mesh axis runs over, the one named last changes fastest.
Arguments:
- positions: float32 [3, 131072], P(None, ('col', 'row')), may hold values from -6 to 6
- velocities: float32 [3, 131072], P(None, ('col', 'row')), may hold values from -4 to 4
- masses: float32 [131072], P(('col', 'row')), may hold values from 7.629395e-09 to 7.6293945e-05
- active_index: int32 [2048], P(('col', 'row')), may hold values from 0 to 4095, as said below
- active_count: int32 [32], P(('col', 'row')), may hold values from 1 to 64, as said below
Outputs:
- accel: float32 [3, 2048], P(None, ('col', 'row'))
- jerk: float32 [3, 2048], P(None, ('col', 'row'))
The draws below stay inside these ranges and needn't reach their ends.
Inputs may be any that keep to these rules, and one draw needn't show every extreme that they name: `active_index`: entries of block b (slots b * 64 to (b + 1) * 64 - 1) index stars of the block of 4096 that block b owns; the entries of one block are distinct. `active_count`: number of used slots of each block, counted from the block's first slot. Some block uses all 64 slots in every draw.
All inputs are finite; a program needn't handle non-finite values.
Results may differ from the reference program's by a relative error of at most 0.0003.
Values sent between devices are 32-bit elements; how exact they have to be, the bound alone decides.
No kernel may reach another device: no remote copies, remote signals or barrier semaphores. Data moves between devices by JAX's collectives and lax.ppermute only.
A program may use at most 64 MiB of HBM per device.

```python
import math
import jax
import jax.numpy as jnp
from jax import lax

STARS_DEV = 4096
ACT_CAP = 64
STARS = 131072
SLOTS = 2048


def draw_active_index(key, part):
    blocks = SLOTS // ACT_CAP
    block_keys = jax.random.split(jax.random.fold_in(key, 11), blocks)

    def one_block(block_key):
        return jax.random.permutation(block_key, STARS_DEV)[:ACT_CAP]
    return jax.vmap(one_block)(block_keys).reshape(SLOTS).astype(jnp.int32)


def draw_active_count(key, part):
    blocks = SLOTS // ACT_CAP
    lowest = max(ACT_CAP // 4, 1)
    first_key = jax.random.fold_in(key, 21)
    second_key = jax.random.fold_in(key, 22)
    third_key = jax.random.fold_in(key, 23)
    first_draw = jax.random.randint(first_key, (blocks,), lowest, ACT_CAP + 1)
    second_draw = jax.random.randint(second_key, (blocks,), lowest, ACT_CAP + 1)
    counts = jnp.maximum(first_draw * second_draw // ACT_CAP, 1)
    chosen = jax.random.randint(third_key, (), 0, blocks)
    counts = jnp.where(jnp.arange(blocks) == chosen, ACT_CAP, counts)
    return counts.astype(jnp.int32)


def level_of(rng, shape, cuts, smallest, top_value):
    factor_of, own = 1.0, jax.random.fold_in(rng, 6)
    for dim, blocks in cuts:
        draws = jnp.exp(jax.random.uniform(jax.random.fold_in(own, dim), (blocks,), jnp.float32, smallest / len(cuts), top_value / len(cuts)))
        factor_of = factor_of * jnp.repeat(draws, shape[dim] // blocks).reshape([-1 if axis == dim else 1 for axis in range(len(shape))])
    return factor_of


def normal_values(key, shape, width, limit, shards=(), kind=jnp.bfloat16):
    array = jax.random.normal(key, shape, jnp.float32) * width
    if len(shards) > 0:
        array = level_of(key, shape, shards, -0.22, 0.18) * array
    return jnp.clip(array, min=-limit, max=limit).astype(kind)


def setup_inputs(seed: int = 0) -> dict:
    keys = jax.random.split(jax.random.key(seed), 6)
    positions = normal_values(keys[0], (3, STARS), 1.0, 6.0, ((1, 32),), jnp.float32)
    velocities = normal_values(keys[1], (3, STARS), 0.5, 4.0, ((1, 32),), jnp.float32)
    masses = jnp.clip(jnp.exp(math.log(7.62939453125e-05) - 9.2103403 * jax.random.uniform(keys[2], (STARS,), jnp.float32) ** level_of(keys[2], (STARS,), ((0, 32),), -0.2, 0.2)), 7.629394893626795e-09, 7.62939453125e-05)
    active_index = draw_active_index(jax.random.fold_in(keys[5], 71), 0)
    active_count = draw_active_count(jax.random.fold_in(keys[5], 71), 0)
    return {"positions": positions, "velocities": velocities, "masses": masses, "active_index": active_index, "active_count": active_count}


SOFTEN = 0.0001

def pair_block(actives, field_piece):
    offset = field_piece[0:3, None, :] - actives[0:3, :, None]
    rel_vel = field_piece[3:6, None, :] - actives[3:6, :, None]
    squared = lax.optimization_barrier(jnp.sum(offset * offset, axis=0)) + SOFTEN
    inverse = 1.0 / squared
    strength = field_piece[6][None, :] * inverse / jnp.sqrt(squared)
    radial = 3.0 * lax.optimization_barrier(jnp.sum(offset * rel_vel, axis=0)) * inverse
    accel_part = lax.optimization_barrier(jnp.sum(strength[None] * offset, axis=2))
    jerk_part = lax.optimization_barrier(jnp.sum(strength[None] * (rel_vel - radial[None] * offset), axis=2))
    return jnp.concatenate([accel_part, jerk_part], axis=0)

def reference(positions, velocities, masses, active_index, active_count):
    slot_ids = jnp.arange(SLOTS, dtype=jnp.int32)
    owner_block = (slot_ids // ACT_CAP).astype(jnp.int32)
    global_index = (owner_block * STARS_DEV + active_index).astype(jnp.int32)
    actives = jnp.concatenate([jnp.take(positions, global_index, axis=1), jnp.take(velocities, global_index, axis=1)], axis=0)
    field_stars = jnp.concatenate([positions, velocities, masses[None, :]], axis=0)
    block_cols = math.gcd(STARS, 2048)
    count_blocks = STARS // block_cols
    pieces = field_stars.reshape(7, count_blocks, block_cols).transpose(1, 0, 2)

    def add_piece(summed, field_piece):
        return (summed + pair_block(actives, field_piece), None)
    summed, unused = lax.scan(add_piece, jnp.zeros((6, SLOTS), jnp.float32), pieces)
    used_slot = slot_ids % ACT_CAP < jnp.take(active_count, owner_block)
    summed = jnp.where(used_slot[None, :], summed, 0.0)
    return (summed[0:3], summed[3:6])
```

```python
import functools

import jax
import jax.numpy as jnp
import numpy as np
from jax import lax
from jax.experimental import pallas as pl
from jax.experimental.pallas import tpu as pltpu
from jax.sharding import PartitionSpec as P

AXES = ("col", "row")
SOFTEN = 0.0001
F32 = jnp.float32
CH = 16
GROUP = 16


def vmem():
    return pl.BlockSpec(memory_space=pltpu.VMEM)


def smem():
    return pl.BlockSpec(memory_space=pltpu.SMEM)


def prepare_kernel(parts, index_ref, count_ref, pos_ref, vel_ref, mass_ref, send_ref, stars_ref):
    slots = index_ref.shape[0]
    stars_ref[0:3, :] = pos_ref[...]
    stars_ref[3:6, :] = vel_ref[...]
    stars_ref[6:7, :] = mass_ref[...]
    stars_ref[7:8, :] = jnp.zeros_like(mass_ref)
    lane = lax.broadcasted_iota(jnp.int32, (8, 128), 1)
    row = lax.broadcasted_iota(jnp.int32, (8, 128), 0)
    picked = jnp.zeros((8, 128), F32)
    for slot in range(slots):
        star = index_ref[slot]
        tile = stars_ref[:, pl.ds(pl.multiple_of((star // 128) * 128, 128), 128)]
        moved = pltpu.roll(tile, (slot - star % 128) % 128, 1)
        picked = jnp.where(lane == slot, moved, picked)
    picked = jnp.where(row == 6, count_ref[0].astype(F32), picked)[:, :slots]

    def fill(part, carry):
        send_ref[part] = picked
        return carry

    lax.fori_loop(0, parts, fill, 0, unroll=8)


def pair_kernel(recv_ref, stars_ref, send_ref, count_smem, offset_smem, act_ref, sum_ref, acc_ref, sem):
    parts, _, slots = recv_ref.shape
    width = stars_ref.shape[1]
    copy = pltpu.make_async_copy(recv_ref.at[:, 6], count_smem, sem)
    copy.start()
    copy.wait()

    def offsets(part, total):
        offset_smem[part] = total
        used = count_smem[part, 0].astype(jnp.int32)
        return total + ((used + 7) // 8) * 8

    total = lax.fori_loop(0, parts, offsets, 0)

    def unpack(group, carry):
        turned = recv_ref[pl.ds(group * GROUP, GROUP)].reshape(GROUP * 8, slots).T
        for k in range(GROUP):
            first = pl.multiple_of(offset_smem[group * GROUP + k], 8)
            act_ref[pl.ds(first, slots), :] = pltpu.roll(turned, (128 - 8 * k) % 128, 1)
        return carry

    lax.fori_loop(0, parts // GROUP, unpack, 0)

    lane = lax.broadcasted_iota(jnp.int32, (CH, 128), 1)

    def collect(chunk):
        rows = pl.ds(pl.multiple_of(chunk * CH, CH), CH)
        sums = jnp.zeros((CH, 128), F32)
        for k in range(6):
            sums = jnp.where(lane == k, jnp.sum(acc_ref[k], axis=1, keepdims=True), sums)
        sum_ref[rows, :] = sums

    def chunk_step(chunk, carry):
        rows = pl.ds(pl.multiple_of(chunk * CH, CH), CH)
        collect(jnp.maximum(chunk - 1, 0))
        own = act_ref[rows, :]
        act = [jnp.broadcast_to(own[:, k : k + 1], (CH, 128)) for k in range(6)]
        acc = [jnp.zeros((CH, 128), F32) for _ in range(9)]
        for j in range(width // 128):
            star = [
                jnp.broadcast_to(stars_ref[k : k + 1, j * 128 : (j + 1) * 128], (CH, 128))
                for k in range(7)
            ]
            dx = [star[k] - act[k] for k in range(3)]
            dv = [star[3 + k] - act[3 + k] for k in range(3)]
            squared = dx[2] * dx[2] + (dx[1] * dx[1] + (dx[0] * dx[0] + SOFTEN))
            root = lax.rsqrt(squared)
            inverse = root * root
            strength = (star[6] * root) * inverse
            dot = dx[0] * dv[0] + dx[1] * dv[1] + dx[2] * dv[2]
            pull = (dot * inverse) * strength
            for k in range(3):
                acc[k] += strength * dx[k]
                acc[3 + k] += strength * dv[k]
                acc[6 + k] += pull * dx[k]
        for k in range(3):
            acc_ref[k] = acc[k]
            acc_ref[3 + k] = acc[3 + k] - 3.0 * acc[6 + k]
        return carry

    chunks = (total + CH - 1) // CH
    lax.fori_loop(0, chunks, chunk_step, 0)
    collect(chunks - 1)

    lane_all = lax.broadcasted_iota(jnp.int32, (slots, 128), 1)

    def pack(group, carry):
        turned = jnp.zeros((slots, 128), F32)
        for k in range(GROUP):
            first = pl.multiple_of(offset_smem[group * GROUP + k], 8)
            moved = pltpu.roll(sum_ref[pl.ds(first, slots), :], 8 * k, 1)
            turned = jnp.where((lane_all >= 8 * k) & (lane_all < 8 * k + 8), moved, turned)
        send_ref[pl.ds(group * GROUP, GROUP)] = turned.T.reshape(GROUP, 8, slots)
        return carry

    lax.fori_loop(0, parts // GROUP, pack, 0)


def finish_kernel(count_ref, recv_ref, accel_ref, jerk_ref):
    parts, _, slots = recv_ref.shape

    def add(part, total):
        return total + recv_ref[part]

    total = lax.fori_loop(1, parts, add, recv_ref[0], unroll=8)
    slot = lax.broadcasted_iota(jnp.int32, (8, slots), 1)
    total = jnp.where(slot < count_ref[0], total, 0.0)
    accel_ref[...] = total[0:3]
    jerk_ref[...] = total[3:6]


def body(parts, positions, velocities, masses, active_index, active_count):
    slots = active_index.shape[0]
    width = positions.shape[1]
    send, stars = pl.pallas_call(
        functools.partial(prepare_kernel, parts),
        out_shape=(
            jax.ShapeDtypeStruct((parts, 8, slots), F32),
            jax.ShapeDtypeStruct((8, width), F32),
        ),
        in_specs=[smem(), smem(), vmem(), vmem(), vmem()],
        out_specs=(vmem(), vmem()),
    )(active_index, active_count, positions, velocities, masses.reshape(1, width))
    received = lax.all_to_all(send, AXES, 0, 0)
    rows = parts * slots + slots
    partial_sums = pl.pallas_call(
        pair_kernel,
        out_shape=jax.ShapeDtypeStruct((parts, 8, slots), F32),
        in_specs=[vmem(), vmem()],
        out_specs=vmem(),
        scratch_shapes=[
            pltpu.SMEM((parts, slots), F32),
            pltpu.SMEM((parts,), jnp.int32),
            pltpu.VMEM((rows, 128), F32),
            pltpu.VMEM((rows, 128), F32),
            pltpu.VMEM((6, CH, 128), F32),
            pltpu.SemaphoreType.DMA,
        ],
        compiler_params=pltpu.CompilerParams(vmem_limit_bytes=48 * 1024 * 1024),
    )(received, stars)
    returned = lax.all_to_all(partial_sums, AXES, 0, 0)
    return pl.pallas_call(
        finish_kernel,
        out_shape=(
            jax.ShapeDtypeStruct((3, slots), F32),
            jax.ShapeDtypeStruct((3, slots), F32),
        ),
        in_specs=[smem(), vmem()],
        out_specs=(vmem(), vmem()),
    )(active_count, returned)


def solution(mesh):
    parts = int(np.prod([mesh.shape[axis] for axis in AXES]))
    return jax.shard_map(
        functools.partial(body, parts),
        mesh=mesh,
        in_specs=(P(None, AXES), P(None, AXES), P(AXES), P(AXES), P(AXES)),
        out_specs=(P(None, AXES), P(None, AXES)),
        check_vma=False,
    )
```

```python
import functools

import jax
import jax.numpy as jnp
import numpy as np
from jax import lax
from jax.experimental import pallas as pl
from jax.experimental.pallas import tpu as pltpu
from jax.sharding import PartitionSpec as P

AXES = ("col", "row")
SOFTEN = 0.0001
F32 = jnp.float32
BF16 = jnp.bfloat16
TILE = 128
CH = 16
BLOCK = 256
UNROLL = 4
PAIRS = ((0, 0), (1, 0), (0, 1), (1, 1), (2, 0), (0, 2))
RAW = 8 * len(PAIRS)
NN = (((1,), (0,)), ((), ()))
NT = (((1,), (1,)), ((), ()))


def vmem():
    return pl.BlockSpec(memory_space=pltpu.VMEM)


def smem():
    return pl.BlockSpec(memory_space=pltpu.SMEM)


def pieces(value):
    first = value.astype(BF16).astype(F32)
    rest = value - first
    second = rest.astype(BF16).astype(F32)
    return first, second, (rest - second).astype(BF16).astype(F32)


def prepare_kernel(parts, index_ref, count_ref, pos_ref, vel_ref, mass_ref, send_ref, pos_out, dot_ref, sum_ref, stars_ref):
    slots = index_ref.shape[0]
    pos, vel, mass = pos_ref[...], vel_ref[...], mass_ref[...]
    width = pos.shape[1]
    ones = jnp.ones_like(mass)
    cross = jnp.sum(pos * vel, axis=0, keepdims=True)
    stars_ref[...] = jnp.concatenate([pos, vel, cross, ones], axis=0)
    pos_out[...] = jnp.concatenate([pos, jnp.zeros((5, width), F32)], axis=0)
    lane = lax.broadcasted_iota(jnp.int32, (8, 128), 1)
    picked = jnp.zeros((8, 128), F32)
    for slot in range(slots):
        star = index_ref[slot]
        tile = stars_ref[:, pl.ds(pl.multiple_of((star // 128) * 128, 128), 128)]
        moved = pltpu.roll(tile, (slot - star % 128) % 128, 1)
        picked = jnp.where(lane == slot, moved, picked)
    picked = jnp.where(lane < slots, picked, count_ref[0].astype(F32))

    def fill(part, carry):
        send_ref[part] = picked
        return carry

    lax.fori_loop(0, parts, fill, 0, unroll=8)
    heavy = 3.0 * mass
    dot_rows = jnp.concatenate([-heavy * vel, -heavy * pos, heavy, heavy * cross], axis=0)
    dots = [piece.astype(BF16) for piece in pieces(dot_rows)]
    for k, (mine, _) in enumerate(PAIRS):
        dot_ref[8 * k : 8 * k + 8, :] = dots[mine]
    dot_ref[RAW:, :] = jnp.zeros((128 - RAW, width), BF16)
    sum_rows = jnp.concatenate([mass * pos, mass * vel, mass, jnp.zeros_like(mass)], axis=0)
    for k, piece in enumerate(pieces(sum_rows)):
        sum_ref[8 * k : 8 * k + 8, :] = piece.astype(BF16)


def pair_kernel(slots, recv_ref, pos_ref, dot_ref, sum_ref, send_ref, count_smem, offset_smem, act_ref, own_ref, pull_ref, res_ref, sem):
    parts = recv_ref.shape[0]
    width = pos_ref.shape[1]
    copy = pltpu.make_async_copy(recv_ref.at[:, 0], count_smem, sem)
    copy.start()
    copy.wait()

    def offsets(part, total):
        offset_smem[part] = total
        used = count_smem[part, 127].astype(jnp.int32)
        return total + ((used + 7) // 8) * 8

    total = lax.fori_loop(0, parts, offsets, 0)

    def unpack(part, carry):
        own = recv_ref[part]
        split = pieces(own)
        rows = [split[theirs] for _, theirs in PAIRS] + [own]
        rows.append(jnp.zeros((128 - 8 * len(rows), 128), F32))
        first = pl.multiple_of(offset_smem[part], 8)
        act_ref[pl.ds(first, slots), :] = jnp.concatenate(rows, axis=0).T[:slots]
        return carry

    lax.fori_loop(0, parts, unpack, 0, unroll=4)

    def tile_step(tile, carry):
        rows = pl.ds(pl.multiple_of(tile * TILE, TILE), TILE)
        act = act_ref[rows, :]
        for k in range(3):
            own_ref[k] = jnp.broadcast_to(act[:, RAW + k : RAW + k + 1], (TILE, 128))
            pull_ref[k] = jnp.zeros((TILE, 128), F32)
        left = act.astype(BF16)

        def block_step(step, sums):
            for block in range(UNROLL):
                cols = pl.ds(pl.multiple_of((step * UNROLL + block) * BLOCK, BLOCK), BLOCK)
                dot = lax.dot_general(left, dot_ref[:, cols], NN, preferred_element_type=F32)
                high, low = [], []
                for chunk in range(TILE // CH):
                    part = slice(chunk * CH, chunk * CH + CH)
                    own = [own_ref[k, part, :] for k in range(3)]
                    acc = [pull_ref[k, part, :] for k in range(3)]
                    highs, lows = [], []
                    for half in range(BLOCK // 128):
                        lanes = pl.ds(pl.multiple_of((step * UNROLL + block) * BLOCK + half * 128, 128), 128)
                        star = [jnp.broadcast_to(pos_ref[k : k + 1, lanes], (CH, 128)) for k in range(3)]
                        dx = [star[k] - own[k] for k in range(3)]
                        squared = dx[2] * dx[2] + (dx[1] * dx[1] + (dx[0] * dx[0] + SOFTEN))
                        root = lax.rsqrt(squared)
                        inverse = root * root
                        cube = root * inverse
                        pull = (dot[part, half * 128 : half * 128 + 128] * inverse) * cube
                        for k in range(3):
                            acc[k] += pull * dx[k]
                        first = cube.astype(BF16)
                        highs.append(first)
                        lows.append((cube - first.astype(F32)).astype(BF16))
                    for k in range(3):
                        pull_ref[k, part, :] = acc[k]
                    high.append(jnp.concatenate(highs, axis=1))
                    low.append(jnp.concatenate(lows, axis=1))
                field = sum_ref[:, cols]
                sums += lax.dot_general(field, jnp.concatenate(high, axis=0), NT, preferred_element_type=F32)
                sums += lax.dot_general(field, jnp.concatenate(low, axis=0), NT, preferred_element_type=F32)
            return sums

        sums = lax.fori_loop(0, width // (BLOCK * UNROLL), block_step, jnp.zeros((24, TILE), F32))
        sums = sums[0:8] + sums[8:16] + sums[16:24]
        pulls = [jnp.sum(pull_ref[k].T, axis=0, keepdims=True) for k in range(3)]
        zero = jnp.zeros((3, TILE), F32)
        sums = jnp.concatenate([sums, *pulls, jnp.zeros((117, TILE), F32)], axis=0).T
        res_ref[rows, :] = sums
        return carry

    lax.fori_loop(0, (total + TILE - 1) // TILE, tile_step, 0)

    def pack(part, carry):
        first = pl.multiple_of(offset_smem[part], 8)
        sums = res_ref[pl.ds(first, slots), :]
        turned = jnp.concatenate([sums, jnp.zeros((128 - slots, 128), F32)], axis=0).T
        own = recv_ref[part]
        result = turned[0:8] - own * turned[6:7]
        send_ref[part] = result - jnp.concatenate([jnp.zeros((3, 128), F32), turned[8:11], jnp.zeros((2, 128), F32)], axis=0)
        return carry

    lax.fori_loop(0, parts, pack, 0, unroll=4)


def finish_kernel(count_ref, recv_ref, accel_ref, jerk_ref):
    parts = recv_ref.shape[0]
    slots = accel_ref.shape[1]

    def add(part, total):
        return total + recv_ref[part]

    total = lax.fori_loop(1, parts, add, recv_ref[0], unroll=8)
    slot = lax.broadcasted_iota(jnp.int32, (8, 128), 1)
    total = jnp.where(slot < count_ref[0], total, 0.0)
    accel_ref[...] = total[0:3, :slots]
    jerk_ref[...] = total[3:6, :slots]


def pair_call(parts, slots, width):
    rows = parts * slots + TILE
    return pl.pallas_call(
        functools.partial(pair_kernel, slots),
        out_shape=jax.ShapeDtypeStruct((parts, 8, 128), F32),
        in_specs=[vmem()] * 4,
        out_specs=vmem(),
        scratch_shapes=[
            pltpu.SMEM((parts, 128), F32),
            pltpu.SMEM((parts,), jnp.int32),
            pltpu.VMEM((rows, 128), F32),
            pltpu.VMEM((3, TILE, 128), F32),
            pltpu.VMEM((3, TILE, 128), F32),
            pltpu.VMEM((rows, 128), F32),
            pltpu.SemaphoreType.DMA,
        ],
        compiler_params=pltpu.CompilerParams(vmem_limit_bytes=48 * 1024 * 1024),
    )


def body(parts, positions, velocities, masses, active_index, active_count):
    slots = active_index.shape[0]
    width = positions.shape[1]
    send, pos, dots, sums = pl.pallas_call(
        functools.partial(prepare_kernel, parts),
        out_shape=(
            jax.ShapeDtypeStruct((parts, 8, 128), F32),
            jax.ShapeDtypeStruct((8, width), F32),
            jax.ShapeDtypeStruct((128, width), BF16),
            jax.ShapeDtypeStruct((24, width), BF16),
        ),
        in_specs=[smem(), smem(), vmem(), vmem(), vmem()],
        out_specs=(vmem(),) * 4,
        scratch_shapes=[pltpu.VMEM((8, width), F32)],
    )(active_index, active_count, positions, velocities, masses.reshape(1, width))
    received = lax.all_to_all(send.reshape(parts * 8, 128), AXES, 0, 0, tiled=True).reshape(parts, 8, 128)
    partial_sums = pair_call(parts, slots, width)(received, pos, dots, sums)
    returned = lax.all_to_all(partial_sums.reshape(parts * 8, 128), AXES, 0, 0, tiled=True).reshape(parts, 8, 128)
    return pl.pallas_call(
        finish_kernel,
        out_shape=(
            jax.ShapeDtypeStruct((3, slots), F32),
            jax.ShapeDtypeStruct((3, slots), F32),
        ),
        in_specs=[smem(), vmem()],
        out_specs=(vmem(), vmem()),
    )(active_count, returned)


def solution(mesh):
    parts = int(np.prod([mesh.shape[axis] for axis in AXES]))
    return jax.shard_map(
        functools.partial(body, parts),
        mesh=mesh,
        in_specs=(P(None, AXES), P(None, AXES), P(AXES), P(AXES), P(AXES)),
        out_specs=(P(None, AXES), P(None, AXES)),
        check_vma=False,
    )
```

```python
import functools

import jax
import jax.numpy as jnp
import numpy as np
from jax import lax
from jax.experimental import pallas as pl
from jax.experimental.pallas import tpu as pltpu
from jax.sharding import PartitionSpec as P

AXES = ("col", "row")
SOFTEN = 0.0001
F32 = jnp.float32
BF16 = jnp.bfloat16
TILE = 128
CH = 16
BLOCK = 256
UNROLL = 16
PAIRS = ((0, 0), (1, 0), (0, 1), (1, 1), (2, 0), (0, 2))
RAW = 8 * len(PAIRS)
DEPTH = 64
NN = (((1,), (0,)), ((), ()))
NT = (((1,), (1,)), ((), ()))


def vmem():
    return pl.BlockSpec(memory_space=pltpu.VMEM)


def smem():
    return pl.BlockSpec(memory_space=pltpu.SMEM)


def pieces(value):
    first = value.astype(BF16).astype(F32)
    rest = value - first
    second = rest.astype(BF16).astype(F32)
    return first, second, (rest - second).astype(BF16).astype(F32)


def prepare_kernel(parts, index_ref, count_ref, pos_ref, vel_ref, send_ref, stars_ref):
    slots = index_ref.shape[0]
    pos, vel = pos_ref[...], vel_ref[...]
    cross = jnp.sum(pos * vel, axis=0, keepdims=True)
    stars_ref[...] = jnp.concatenate([pos, cross, vel, cross], axis=0)
    lane = lax.broadcasted_iota(jnp.int32, (8, 128), 1)
    picked = jnp.zeros((8, 128), F32)
    for slot in range(slots):
        star = index_ref[slot]
        tile = stars_ref[:, pl.ds(pl.multiple_of((star // 128) * 128, 128), 128)]
        moved = pltpu.roll(tile, (slot - star % 128) % 128, 1)
        picked = jnp.where(lane == slot, moved, picked)
    row = lax.broadcasted_iota(jnp.int32, (4, 128), 0)
    upper = jnp.where(row == 3, count_ref[0].astype(F32), pltpu.roll(picked[4:8], slots, 1))
    payload = jnp.where(lane[0:4] < slots, picked[0:4], upper)

    def fill(part, carry):
        send_ref[part] = payload
        return carry

    lax.fori_loop(0, parts, fill, 0, unroll=8)


def pair_kernel(slots, recv_ref, pos_ref, vel_ref, mass_ref, send_ref, count_smem, offset_smem, dot_ref, sum_ref, slot_ref, own_ref, pull_ref, res_ref, sem):
    parts = recv_ref.shape[0]
    width = pos_ref.shape[1]
    copy = pltpu.make_async_copy(recv_ref.at[:, 3], count_smem, sem)
    copy.start()

    def star_step(step, carry):
        cols = pl.ds(pl.multiple_of(step * 512, 512), 512)
        pos, vel, mass = pos_ref[:, cols], vel_ref[:, cols], mass_ref[:, cols]
        heavy = 3.0 * mass
        cross = jnp.sum(pos * vel, axis=0, keepdims=True)
        dots = pieces(jnp.concatenate([-heavy * vel, heavy, -heavy * pos, heavy * cross], axis=0))
        for k, (mine, _) in enumerate(PAIRS):
            dot_ref[8 * k : 8 * k + 8, cols] = dots[mine].astype(BF16)
        dot_ref[RAW:DEPTH, cols] = jnp.zeros((DEPTH - RAW, 512), BF16)
        sums = pieces(jnp.concatenate([mass * pos, mass, mass * vel, jnp.zeros_like(mass)], axis=0))
        for k in range(3):
            sum_ref[8 * k : 8 * k + 8, cols] = sums[k].astype(BF16)
        return carry

    lax.fori_loop(0, width // 512, star_step, 0)
    copy.wait()

    lane = lax.broadcasted_iota(jnp.int32, (8, 128), 1)
    row = lax.broadcasted_iota(jnp.int32, (8, 128), 0)

    def gather(part, total):
        offset_smem[part] = total
        raw = recv_ref[part]
        own = jnp.concatenate([raw, pltpu.roll(raw, 128 - slots, 1)], axis=0)
        own = jnp.where(row == 7, 1.0, own)
        tile, start = total // 128, total % 128
        moved = pltpu.roll(own, start, 1)
        slot_ref[tile] = jnp.where(lane < start, slot_ref[tile], moved)
        slot_ref[tile + 1] = moved
        return total + count_smem[part, 127].astype(jnp.int32)

    total = lax.fori_loop(0, parts, gather, 0, unroll=8)

    def tile_step(tile, carry):
        slot = slot_ref[tile]
        split = pieces(slot)
        rows = [split[theirs] for _, theirs in PAIRS] + [slot, jnp.zeros((DEPTH - RAW - 8, TILE), F32)]
        act = jnp.concatenate(rows, axis=0).T
        for k in range(3):
            own_ref[k] = jnp.broadcast_to(act[:, RAW + k : RAW + k + 1], (TILE, 128))
            pull_ref[k] = jnp.zeros((TILE, 128), F32)
        left = act.astype(BF16)

        def block_step(step, sums):
            for block in range(UNROLL):
                cols = pl.ds(pl.multiple_of((step * UNROLL + block) * BLOCK, BLOCK), BLOCK)
                dot = lax.dot_general(left, dot_ref[:, cols], NN, preferred_element_type=F32)
                high, low = [], []
                for chunk in range(TILE // CH):
                    part = slice(chunk * CH, chunk * CH + CH)
                    own = [own_ref[k, part, :] for k in range(3)]
                    acc = [pull_ref[k, part, :] for k in range(3)]
                    highs, lows = [], []
                    for half in range(BLOCK // 128):
                        lanes = pl.ds(pl.multiple_of((step * UNROLL + block) * BLOCK + half * 128, 128), 128)
                        star = [jnp.broadcast_to(pos_ref[k : k + 1, lanes], (CH, 128)) for k in range(3)]
                        dx = [star[k] - own[k] for k in range(3)]
                        squared = dx[2] * dx[2] + (dx[1] * dx[1] + (dx[0] * dx[0] + SOFTEN))
                        root = lax.rsqrt(squared)
                        inverse = root * root
                        cube = root * inverse
                        pull = (dot[part, half * 128 : half * 128 + 128] * inverse) * cube
                        for k in range(3):
                            acc[k] += pull * dx[k]
                        first = cube.astype(BF16)
                        highs.append(first)
                        lows.append((cube - first.astype(F32)).astype(BF16))
                    for k in range(3):
                        pull_ref[k, part, :] = acc[k]
                    high.append(jnp.concatenate(highs, axis=1))
                    low.append(jnp.concatenate(lows, axis=1))
                field = sum_ref[:, cols]
                sums += lax.dot_general(field, jnp.concatenate(high, axis=0), NT, preferred_element_type=F32)
                sums += lax.dot_general(field, jnp.concatenate(low, axis=0), NT, preferred_element_type=F32)
            return sums

        sums = lax.fori_loop(0, width // (BLOCK * UNROLL), block_step, jnp.zeros((24, TILE), F32))
        sums = sums[0:8] + sums[8:16] + sums[16:24]
        pulls = [jnp.sum(pull_ref[k].T, axis=0, keepdims=True) for k in range(3)]
        pulls = jnp.concatenate([jnp.zeros((4, TILE), F32), *pulls, jnp.zeros((1, TILE), F32)], axis=0)
        res_ref[tile] = sums - slot * sums[3:4] - pulls
        return carry

    lax.fori_loop(0, (total + TILE - 1) // TILE, tile_step, 0)

    def spread(part, carry):
        first = offset_smem[part]
        tile, start = first // 128, first % 128
        back = (128 - start) % 128
        moved = jnp.where(lane < 128 - start, pltpu.roll(res_ref[tile], back, 1), pltpu.roll(res_ref[tile + 1], back, 1))
        send_ref[part] = jnp.where(lane[0:4] < slots, moved[0:4], pltpu.roll(moved[4:8], slots, 1))
        return carry

    lax.fori_loop(0, parts, spread, 0, unroll=8)


def finish_kernel(count_ref, recv_ref, accel_ref, jerk_ref):
    parts = recv_ref.shape[0]
    slots = accel_ref.shape[1]

    def add(part, total):
        return total + recv_ref[part]

    total = lax.fori_loop(1, parts, add, recv_ref[0], unroll=8)
    lane = lax.broadcasted_iota(jnp.int32, (4, 128), 1)
    total = jnp.where(lane % slots < count_ref[0], total, 0.0)
    accel_ref[...] = total[0:3, :slots]
    jerk_ref[...] = total[0:3, slots : 2 * slots]


def pair_call(parts, slots, width):
    tiles = (parts * slots) // TILE + 2
    return pl.pallas_call(
        functools.partial(pair_kernel, slots),
        out_shape=jax.ShapeDtypeStruct((parts, 4, 128), F32),
        in_specs=[vmem()] * 4,
        out_specs=vmem(),
        scratch_shapes=[
            pltpu.SMEM((parts, 128), F32),
            pltpu.SMEM((parts,), jnp.int32),
            pltpu.VMEM((DEPTH, width), BF16),
            pltpu.VMEM((24, width), BF16),
            pltpu.VMEM((tiles, 8, 128), F32),
            pltpu.VMEM((3, TILE, 128), F32),
            pltpu.VMEM((3, TILE, 128), F32),
            pltpu.VMEM((tiles, 8, 128), F32),
            pltpu.SemaphoreType.DMA,
        ],
        compiler_params=pltpu.CompilerParams(vmem_limit_bytes=48 * 1024 * 1024),
    )


def body(parts, positions, velocities, masses, active_index, active_count):
    slots = active_index.shape[0]
    width = positions.shape[1]
    send = pl.pallas_call(
        functools.partial(prepare_kernel, parts),
        out_shape=jax.ShapeDtypeStruct((parts, 4, 128), F32),
        in_specs=[smem(), smem(), vmem(), vmem()],
        out_specs=vmem(),
        scratch_shapes=[pltpu.VMEM((8, width), F32)],
    )(active_index, active_count, positions, velocities)
    received = lax.all_to_all(send, AXES, 0, 0, tiled=True)
    partial_sums = pair_call(parts, slots, width)(received, positions, velocities, masses.reshape(1, width))
    returned = lax.all_to_all(partial_sums, AXES, 0, 0, tiled=True)
    return pl.pallas_call(
        finish_kernel,
        out_shape=(
            jax.ShapeDtypeStruct((3, slots), F32),
            jax.ShapeDtypeStruct((3, slots), F32),
        ),
        in_specs=[smem(), vmem()],
        out_specs=(vmem(), vmem()),
    )(active_count, returned)


def solution(mesh):
    parts = int(np.prod([mesh.shape[axis] for axis in AXES]))
    return jax.shard_map(
        functools.partial(body, parts),
        mesh=mesh,
        in_specs=(P(None, AXES), P(None, AXES), P(AXES), P(AXES), P(AXES)),
        out_specs=(P(None, AXES), P(None, AXES)),
        check_vma=False,
    )
```

```python
import functools

import jax
import jax.numpy as jnp
import numpy as np
from jax import lax
from jax.experimental import pallas as pl
from jax.experimental.pallas import tpu as pltpu
from jax.sharding import PartitionSpec as P

AXES = ("col", "row")
SOFTEN = 0.0001
MARK = 8.0
F32 = jnp.float32
BF16 = jnp.bfloat16
TILE = 128
CH = 16
BLOCK = 256
UNROLL = 16
PAIRS = ((0, 0), (1, 0), (0, 1), (1, 1), (2, 0), (0, 2))
RAW = 8 * len(PAIRS)
DEPTH = 64
NN = (((1,), (0,)), ((), ()))
NT = (((1,), (1,)), ((), ()))


def vmem():
    return pl.BlockSpec(memory_space=pltpu.VMEM)


def smem():
    return pl.BlockSpec(memory_space=pltpu.SMEM)


def hbm():
    return pl.BlockSpec(memory_space=pltpu.HBM)


def pieces(value):
    first = value.astype(BF16).astype(F32)
    rest = value - first
    second = rest.astype(BF16).astype(F32)
    return first, second, (rest - second).astype(BF16).astype(F32)


def prepare_kernel(parts, index_ref, count_ref, pos_hbm, vel_hbm, send_ref, pos_ref, vel_ref, sems):
    slots = index_ref.shape[0]
    copies = [
        pltpu.make_async_copy(pos_hbm, pos_ref, sems.at[0]),
        pltpu.make_async_copy(vel_hbm, vel_ref, sems.at[1]),
    ]
    for copy in copies:
        copy.start()
    for copy in copies:
        copy.wait()
    lane = lax.broadcasted_iota(jnp.int32, (3, 128), 1)
    picked = jnp.zeros((3, 128), F32)
    for slot in range(slots):
        star = index_ref[slot]
        tile = pl.ds(pl.multiple_of((star >> 7) << 7, 128), 128)
        shift = slot - star
        moved = pltpu.roll(pos_ref[:, tile], shift & 127, 1)
        picked = jnp.where(lane == slot, moved, picked)
        moved = pltpu.roll(vel_ref[:, tile], (shift + slots) & 127, 1)
        picked = jnp.where(lane == slot + slots, moved, picked)
    row = lax.broadcasted_iota(jnp.int32, (3, 128), 0)
    count = count_ref[0]
    mark = (row == 0) & (lane == slots - 1) & (count < slots)
    picked = jnp.where(mark, MARK + count.astype(F32), picked)

    def fill(part, carry):
        for k in range(3):
            send_ref[part, :, 128 * k : 128 * k + 128] = picked[k : k + 1]
        return carry

    lax.fori_loop(0, parts, fill, 0, unroll=8)


def pair_kernel(slots, recv_ref, pos_ref, vel_ref, mass_ref, send_ref, count_smem, offset_smem, dot_ref, sum_ref, slot_ref, own_ref, pull_ref, res_ref, sem):
    parts = recv_ref.shape[0]
    width = pos_ref.shape[1]
    copy = pltpu.make_async_copy(recv_ref.at[:, 0, 0:128], count_smem, sem)
    copy.start()

    def star_step(step, carry):
        cols = pl.ds(pl.multiple_of(step * 512, 512), 512)
        pos, vel, mass = pos_ref[:, cols], vel_ref[:, cols], mass_ref[:, cols]
        heavy = 3.0 * mass
        cross = jnp.sum(pos * vel, axis=0, keepdims=True)
        dots = pieces(jnp.concatenate([-heavy * vel, heavy, -heavy * pos, heavy * cross], axis=0))
        for k, (mine, _) in enumerate(PAIRS):
            dot_ref[8 * k : 8 * k + 8, cols] = dots[mine].astype(BF16)
        dot_ref[RAW:DEPTH, cols] = jnp.zeros((DEPTH - RAW, 512), BF16)
        sums = pieces(jnp.concatenate([mass * pos, mass, mass * vel, jnp.zeros_like(mass)], axis=0))
        for k in range(3):
            sum_ref[8 * k : 8 * k + 8, cols] = sums[k].astype(BF16)
        return carry

    lax.fori_loop(0, width // 512, star_step, 0)
    copy.wait()

    lane = lax.broadcasted_iota(jnp.int32, (8, 128), 1)
    row = lax.broadcasted_iota(jnp.int32, (8, 128), 0)

    def gather(part, total):
        offset_smem[part] = total
        raw = [recv_ref[part, :, 128 * k : 128 * k + 128] for k in range(3)]
        raw = jnp.concatenate([*raw, raw[0]], axis=0)
        own = jnp.concatenate([raw, pltpu.roll(raw, 128 - slots, 1)], axis=0)
        tile, start = total >> 7, total & 127
        moved = pltpu.roll(own, start, 1)
        slot_ref[tile] = jnp.where(lane < start, slot_ref[tile], moved)
        slot_ref[tile + 1] = moved
        last = count_smem[part, slots - 1]
        return total + jnp.where(last < MARK, slots, (last - MARK).astype(jnp.int32))

    total = lax.fori_loop(0, parts, gather, 0, unroll=8)

    def tile_step(tile, carry):
        slot = slot_ref[tile]
        cross = jnp.sum(slot[0:3] * slot[4:7], axis=0, keepdims=True)
        slot = jnp.where(row == 7, 1.0, jnp.where(row == 3, cross, slot))
        split = pieces(slot)
        rows = [split[theirs] for _, theirs in PAIRS] + [slot, jnp.zeros((DEPTH - RAW - 8, TILE), F32)]
        act = jnp.concatenate(rows, axis=0).T
        for k in range(3):
            own_ref[k] = jnp.broadcast_to(act[:, RAW + k : RAW + k + 1], (TILE, 128))
            pull_ref[k] = jnp.zeros((TILE, 128), F32)
        left = act.astype(BF16)

        def block_step(step, sums):
            for block in range(UNROLL):
                cols = pl.ds(pl.multiple_of((step * UNROLL + block) * BLOCK, BLOCK), BLOCK)
                dot = lax.dot_general(left, dot_ref[:, cols], NN, preferred_element_type=F32)
                high, low = [], []
                for chunk in range(TILE // CH):
                    part = slice(chunk * CH, chunk * CH + CH)
                    own = [own_ref[k, part, :] for k in range(3)]
                    acc = [pull_ref[k, part, :] for k in range(3)]
                    highs, lows = [], []
                    for half in range(BLOCK // 128):
                        lanes = pl.ds(pl.multiple_of((step * UNROLL + block) * BLOCK + half * 128, 128), 128)
                        star = [jnp.broadcast_to(pos_ref[k : k + 1, lanes], (CH, 128)) for k in range(3)]
                        dx = [star[k] - own[k] for k in range(3)]
                        squared = dx[2] * dx[2] + (dx[1] * dx[1] + (dx[0] * dx[0] + SOFTEN))
                        root = lax.rsqrt(squared)
                        inverse = root * root
                        cube = root * inverse
                        pull = (dot[part, half * 128 : half * 128 + 128] * inverse) * cube
                        for k in range(3):
                            acc[k] += pull * dx[k]
                        first = cube.astype(BF16)
                        highs.append(first)
                        lows.append((cube - first.astype(F32)).astype(BF16))
                    for k in range(3):
                        pull_ref[k, part, :] = acc[k]
                    high.append(jnp.concatenate(highs, axis=1))
                    low.append(jnp.concatenate(lows, axis=1))
                field = sum_ref[:, cols]
                sums += lax.dot_general(field, jnp.concatenate(high + low, axis=0), NT, preferred_element_type=F32)
            return sums

        sums = lax.fori_loop(0, width // (BLOCK * UNROLL), block_step, jnp.zeros((24, 2 * TILE), F32))
        sums = sums[:, :TILE] + sums[:, TILE:]
        sums = sums[0:8] + sums[8:16] + sums[16:24]
        pulls = [jnp.sum(pull_ref[k].T, axis=0, keepdims=True) for k in range(3)]
        pulls = jnp.concatenate([jnp.zeros((4, TILE), F32), *pulls, jnp.zeros((1, TILE), F32)], axis=0)
        res_ref[tile] = sums - slot * sums[3:4] - pulls
        return carry

    lax.fori_loop(0, (total + TILE - 1) // TILE, tile_step, 0)

    def spread(part, carry):
        first = offset_smem[part]
        tile, start = first >> 7, first & 127
        back = (128 - start) & 127
        moved = jnp.where(lane < 128 - start, pltpu.roll(res_ref[tile], back, 1), pltpu.roll(res_ref[tile + 1], back, 1))
        moved = jnp.where(lane[0:4] < slots, moved[0:4], pltpu.roll(moved[4:8], slots, 1))
        for k in range(3):
            send_ref[part, :, 128 * k : 128 * k + 128] = moved[k : k + 1]
        return carry

    lax.fori_loop(0, parts, spread, 0, unroll=8)


def finish_kernel(count_ref, recv_ref, accel_ref, jerk_ref):
    slots = accel_ref.shape[1]
    total = jnp.sum(recv_ref[...], axis=0)
    for k in range(3):
        row = total[:, 128 * k : 128 * k + 128]
        lane = lax.broadcasted_iota(jnp.int32, row.shape, 1)
        row = jnp.where(lane % slots < count_ref[0], row, 0.0)
        accel_ref[k : k + 1, :] = row[:, :slots]
        jerk_ref[k : k + 1, :] = row[:, slots : 2 * slots]


def pair_call(parts, slots, width):
    tiles = (parts * slots) // TILE + 2
    return pl.pallas_call(
        functools.partial(pair_kernel, slots),
        out_shape=jax.ShapeDtypeStruct((parts, 1, 384), F32),
        in_specs=[vmem()] * 4,
        out_specs=vmem(),
        scratch_shapes=[
            pltpu.SMEM((parts, 128), F32),
            pltpu.SMEM((parts,), jnp.int32),
            pltpu.VMEM((DEPTH, width), BF16),
            pltpu.VMEM((24, width), BF16),
            pltpu.VMEM((tiles, 8, 128), F32),
            pltpu.VMEM((3, TILE, 128), F32),
            pltpu.VMEM((3, TILE, 128), F32),
            pltpu.VMEM((tiles, 8, 128), F32),
            pltpu.SemaphoreType.DMA,
        ],
        compiler_params=pltpu.CompilerParams(vmem_limit_bytes=48 * 1024 * 1024),
    )


def body(parts, positions, velocities, masses, active_index, active_count):
    slots = active_index.shape[0]
    width = positions.shape[1]
    send = pl.pallas_call(
        functools.partial(prepare_kernel, parts),
        out_shape=jax.ShapeDtypeStruct((parts, 1, 384), F32),
        in_specs=[smem(), smem(), hbm(), hbm()],
        out_specs=vmem(),
        scratch_shapes=[
            pltpu.VMEM((3, width), F32),
            pltpu.VMEM((3, width), F32),
            pltpu.SemaphoreType.DMA((2,)),
        ],
        compiler_params=pltpu.CompilerParams(vmem_limit_bytes=16 * 1024 * 1024),
    )(active_index, active_count, positions, velocities)
    received = lax.all_to_all(send, AXES, 0, 0, tiled=True)
    partial_sums = pair_call(parts, slots, width)(received, positions, velocities, masses.reshape(1, width))
    returned = lax.all_to_all(partial_sums, AXES, 0, 0, tiled=True)
    return pl.pallas_call(
        finish_kernel,
        out_shape=(
            jax.ShapeDtypeStruct((3, slots), F32),
            jax.ShapeDtypeStruct((3, slots), F32),
        ),
        in_specs=[smem(), vmem()],
        out_specs=(vmem(), vmem()),
        compiler_params=pltpu.CompilerParams(vmem_limit_bytes=16 * 1024 * 1024),
    )(active_count, returned)


def solution(mesh):
    parts = int(np.prod([mesh.shape[axis] for axis in AXES]))
    return jax.shard_map(
        functools.partial(body, parts),
        mesh=mesh,
        in_specs=(P(None, AXES), P(None, AXES), P(AXES), P(AXES), P(AXES)),
        out_specs=(P(None, AXES), P(None, AXES)),
        check_vma=False,
    )
```

```python
import functools

import jax
import jax.numpy as jnp
import numpy as np
from jax import lax
from jax.experimental import pallas as pl
from jax.experimental.pallas import tpu as pltpu
from jax.sharding import PartitionSpec as P

AXES = ("col", "row")
SOFTEN = 0.0001
MARK = 8.0
F32 = jnp.float32
BF16 = jnp.bfloat16
TILE = 128
CH = 16
BLOCK = 256
UNROLL = 16
PAIRS = ((0, 0), (1, 0), (0, 1), (1, 1), (2, 0), (0, 2))
RAW = 8 * len(PAIRS)
DEPTH = 64
NN = (((1,), (0,)), ((), ()))
NT = (((1,), (1,)), ((), ()))


def vmem():
    return pl.BlockSpec(memory_space=pltpu.VMEM)


def hbm():
    return pl.BlockSpec(memory_space=pltpu.HBM)


def pieces(value):
    first = value.astype(BF16).astype(F32)
    rest = value - first
    second = rest.astype(BF16).astype(F32)
    return first, second, (rest - second).astype(BF16).astype(F32)


def prepare_kernel(parts, index_hbm, count_ref, pos_hbm, vel_hbm, send_ref, index_ref, pos_ref, vel_ref, sems):
    slots = index_ref.shape[0]
    copies = [
        pltpu.make_async_copy(pos_hbm, pos_ref, sems.at[0]),
        pltpu.make_async_copy(vel_hbm, vel_ref, sems.at[1]),
        pltpu.make_async_copy(index_hbm, index_ref, sems.at[2]),
    ]
    for copy in copies:
        copy.start()
    for copy in copies:
        copy.wait()
    lane = lax.broadcasted_iota(jnp.int32, (3, 128), 1)
    picked = jnp.zeros((3, 128), F32)
    for slot in range(slots):
        star = index_ref[slot]
        tile = pl.ds(pl.multiple_of((star >> 7) << 7, 128), 128)
        shift = slot - star
        moved = pltpu.roll(pos_ref[:, tile], shift & 127, 1)
        picked = jnp.where(lane == slot, moved, picked)
        moved = pltpu.roll(vel_ref[:, tile], (shift + slots) & 127, 1)
        picked = jnp.where(lane == slot + slots, moved, picked)
    row = lax.broadcasted_iota(jnp.int32, (3, 128), 0)
    count = count_ref[...]
    mark = (row == 0) & (lane == slots - 1) & (count < slots)
    picked = jnp.where(mark, MARK + count.astype(F32), picked)

    def fill(part, carry):
        for k in range(3):
            send_ref[part, :, 128 * k : 128 * k + 128] = picked[k : k + 1]
        return carry

    lax.fori_loop(0, parts, fill, 0, unroll=8)


def pair_kernel(slots, recv_ref, pos_ref, vel_ref, mass_ref, send_ref, count_smem, offset_smem, dot_ref, sum_ref, slot_ref, own_ref, pull_ref, res_ref, sem):
    parts = recv_ref.shape[0]
    width = pos_ref.shape[1]
    copy = pltpu.make_async_copy(recv_ref.at[:, 0, 0:128], count_smem, sem)
    copy.start()

    def star_step(step, carry):
        cols = pl.ds(pl.multiple_of(step * 512, 512), 512)
        pos, vel, mass = pos_ref[:, cols], vel_ref[:, cols], mass_ref[:, cols]
        heavy = 3.0 * mass
        cross = jnp.sum(pos * vel, axis=0, keepdims=True)
        dots = pieces(jnp.concatenate([-heavy * vel, heavy, -heavy * pos, heavy * cross], axis=0))
        for k, (mine, _) in enumerate(PAIRS):
            dot_ref[8 * k : 8 * k + 8, cols] = dots[mine].astype(BF16)
        dot_ref[RAW:DEPTH, cols] = jnp.zeros((DEPTH - RAW, 512), BF16)
        sums = pieces(jnp.concatenate([mass * pos, mass, mass * vel, jnp.zeros_like(mass)], axis=0))
        for k in range(3):
            sum_ref[8 * k : 8 * k + 8, cols] = sums[k].astype(BF16)
        return carry

    lax.fori_loop(0, width // 512, star_step, 0)
    copy.wait()

    lane = lax.broadcasted_iota(jnp.int32, (8, 128), 1)
    row = lax.broadcasted_iota(jnp.int32, (8, 128), 0)

    def gather(part, total):
        offset_smem[part] = total
        raw = [recv_ref[part, :, 128 * k : 128 * k + 128] for k in range(3)]
        raw = jnp.concatenate([*raw, raw[0]], axis=0)
        own = jnp.concatenate([raw, pltpu.roll(raw, 128 - slots, 1)], axis=0)
        tile, start = total >> 7, total & 127
        moved = pltpu.roll(own, start, 1)
        slot_ref[tile] = jnp.where(lane < start, slot_ref[tile], moved)
        slot_ref[tile + 1] = moved
        last = count_smem[part, slots - 1]
        return total + jnp.where(last < MARK, slots, (last - MARK).astype(jnp.int32))

    total = lax.fori_loop(0, parts, gather, 0, unroll=8)

    def tile_step(tile, carry):
        slot = slot_ref[tile]
        cross = jnp.sum(slot[0:3] * slot[4:7], axis=0, keepdims=True)
        slot = jnp.where(row == 7, 1.0, jnp.where(row == 3, cross, slot))
        split = pieces(slot)
        rows = [split[theirs] for _, theirs in PAIRS] + [slot, jnp.zeros((DEPTH - RAW - 8, TILE), F32)]
        act = jnp.concatenate(rows, axis=0).T
        for k in range(3):
            own_ref[k] = jnp.broadcast_to(act[:, RAW + k : RAW + k + 1], (TILE, 128))
            pull_ref[k] = jnp.zeros((TILE, 128), F32)
        left = act.astype(BF16)

        def block_step(step, sums):
            for block in range(UNROLL):
                cols = pl.ds(pl.multiple_of((step * UNROLL + block) * BLOCK, BLOCK), BLOCK)
                dot = lax.dot_general(left, dot_ref[:, cols], NN, preferred_element_type=F32)
                high, low = [], []
                for chunk in range(TILE // CH):
                    part = slice(chunk * CH, chunk * CH + CH)
                    own = [own_ref[k, part, :] for k in range(3)]
                    acc = [pull_ref[k, part, :] for k in range(3)]
                    highs, lows = [], []
                    for half in range(BLOCK // 128):
                        lanes = pl.ds(pl.multiple_of((step * UNROLL + block) * BLOCK + half * 128, 128), 128)
                        star = [jnp.broadcast_to(pos_ref[k : k + 1, lanes], (CH, 128)) for k in range(3)]
                        dx = [star[k] - own[k] for k in range(3)]
                        squared = dx[2] * dx[2] + (dx[1] * dx[1] + (dx[0] * dx[0] + SOFTEN))
                        root = lax.rsqrt(squared)
                        inverse = root * root
                        cube = root * inverse
                        pull = (dot[part, half * 128 : half * 128 + 128] * inverse) * cube
                        for k in range(3):
                            acc[k] += pull * dx[k]
                        first = cube.astype(BF16)
                        highs.append(first)
                        lows.append((cube - first.astype(F32)).astype(BF16))
                    for k in range(3):
                        pull_ref[k, part, :] = acc[k]
                    high.append(jnp.concatenate(highs, axis=1))
                    low.append(jnp.concatenate(lows, axis=1))
                field = sum_ref[:, cols]
                sums += lax.dot_general(field, jnp.concatenate(high + low, axis=0), NT, preferred_element_type=F32)
            return sums

        sums = lax.fori_loop(0, width // (BLOCK * UNROLL), block_step, jnp.zeros((24, 2 * TILE), F32))
        sums = sums[:, :TILE] + sums[:, TILE:]
        sums = sums[0:8] + sums[8:16] + sums[16:24]
        pulls = [jnp.sum(pull_ref[k].T, axis=0, keepdims=True) for k in range(3)]
        pulls = jnp.concatenate([jnp.zeros((4, TILE), F32), *pulls, jnp.zeros((1, TILE), F32)], axis=0)
        res_ref[tile] = sums - slot * sums[3:4] - pulls
        return carry

    lax.fori_loop(0, (total + TILE - 1) // TILE, tile_step, 0)

    def spread(part, carry):
        first = offset_smem[part]
        tile, start = first >> 7, first & 127
        back = (128 - start) & 127
        moved = jnp.where(lane < 128 - start, pltpu.roll(res_ref[tile], back, 1), pltpu.roll(res_ref[tile + 1], back, 1))
        moved = jnp.where(lane[0:4] < slots, moved[0:4], pltpu.roll(moved[4:8], slots, 1))
        for k in range(3):
            send_ref[part, :, 128 * k : 128 * k + 128] = moved[k : k + 1]
        return carry

    lax.fori_loop(0, parts, spread, 0, unroll=8)


def finish_kernel(count_ref, recv_ref, accel_ref, jerk_ref):
    slots = accel_ref.shape[1]
    total = jnp.sum(recv_ref[...], axis=0)
    for k in range(3):
        row = total[:, 128 * k : 128 * k + 128]
        lane = lax.broadcasted_iota(jnp.int32, row.shape, 1)
        row = jnp.where(lane % slots < count_ref[...], row, 0.0)
        accel_ref[k : k + 1, :] = row[:, :slots]
        jerk_ref[k : k + 1, :] = row[:, slots : 2 * slots]


def pair_call(parts, slots, width):
    tiles = (parts * slots) // TILE + 2
    return pl.pallas_call(
        functools.partial(pair_kernel, slots),
        out_shape=jax.ShapeDtypeStruct((parts, 1, 384), F32),
        in_specs=[vmem()] * 4,
        out_specs=vmem(),
        scratch_shapes=[
            pltpu.SMEM((parts, 128), F32),
            pltpu.SMEM((parts,), jnp.int32),
            pltpu.VMEM((DEPTH, width), BF16),
            pltpu.VMEM((24, width), BF16),
            pltpu.VMEM((tiles, 8, 128), F32),
            pltpu.VMEM((3, TILE, 128), F32),
            pltpu.VMEM((3, TILE, 128), F32),
            pltpu.VMEM((tiles, 8, 128), F32),
            pltpu.SemaphoreType.DMA,
        ],
        compiler_params=pltpu.CompilerParams(vmem_limit_bytes=48 * 1024 * 1024),
    )


def body(parts, positions, velocities, masses, active_index, active_count):
    slots = active_index.shape[0]
    width = positions.shape[1]
    send = pl.pallas_call(
        functools.partial(prepare_kernel, parts),
        out_shape=jax.ShapeDtypeStruct((parts, 1, 384), F32),
        in_specs=[hbm(), vmem(), hbm(), hbm()],
        out_specs=vmem(),
        scratch_shapes=[
            pltpu.SMEM((slots,), jnp.int32),
            pltpu.VMEM((3, width), F32),
            pltpu.VMEM((3, width), F32),
            pltpu.SemaphoreType.DMA((3,)),
        ],
        compiler_params=pltpu.CompilerParams(vmem_limit_bytes=16 * 1024 * 1024),
    )(
        pltpu.with_memory_space_constraint(active_index, pltpu.HBM),
        active_count.reshape(1, 1),
        pltpu.with_memory_space_constraint(positions, pltpu.HBM),
        pltpu.with_memory_space_constraint(velocities, pltpu.HBM),
    )
    received = lax.all_to_all(send, AXES, 0, 0, tiled=True)
    partial_sums = pair_call(parts, slots, width)(received, positions, velocities, masses.reshape(1, width))
    returned = lax.all_to_all(partial_sums, AXES, 0, 0, tiled=True)
    return pl.pallas_call(
        finish_kernel,
        out_shape=(
            jax.ShapeDtypeStruct((3, slots), F32),
            jax.ShapeDtypeStruct((3, slots), F32),
        ),
        in_specs=[vmem(), vmem()],
        out_specs=(vmem(), vmem()),
        compiler_params=pltpu.CompilerParams(vmem_limit_bytes=16 * 1024 * 1024),
    )(active_count.reshape(1, 1), returned)


def solution(mesh):
    parts = int(np.prod([mesh.shape[axis] for axis in AXES]))
    return jax.shard_map(
        functools.partial(body, parts),
        mesh=mesh,
        in_specs=(P(None, AXES), P(None, AXES), P(AXES), P(AXES), P(AXES)),
        out_specs=(P(None, AXES), P(None, AXES)),
        check_vma=False,
    )
```

```python
import functools

import jax
import jax.numpy as jnp
import numpy as np
from jax import lax
from jax.experimental import pallas as pl
from jax.experimental.pallas import tpu as pltpu
from jax.sharding import PartitionSpec as P

AXES = ("col", "row")
SOFTEN = 0.0001
MARK = 8.0
F32 = jnp.float32
BF16 = jnp.bfloat16
TILE = 128
CH = 16
BLOCK = 256
UNROLL = 16
PAIRS = ((0, 0), (1, 0), (0, 1), (1, 1), (2, 0), (0, 2))
RAW = 8 * len(PAIRS)
DEPTH = 64
NN = (((1,), (0,)), ((), ()))
NT = (((1,), (1,)), ((), ()))


def vmem():
    return pl.BlockSpec(memory_space=pltpu.VMEM)


def hbm():
    return pl.BlockSpec(memory_space=pltpu.HBM)


def pieces(value):
    first = value.astype(BF16).astype(F32)
    rest = value - first
    second = rest.astype(BF16).astype(F32)
    return first, second, (rest - second).astype(BF16).astype(F32)


def prepare_kernel(parts, index_hbm, count_ref, pos_hbm, vel_hbm, send_ref, index_ref, pos_ref, vel_ref, sems):
    slots = index_ref.shape[0]
    copies = [
        pltpu.make_async_copy(pos_hbm, pos_ref, sems.at[0]),
        pltpu.make_async_copy(vel_hbm, vel_ref, sems.at[1]),
        pltpu.make_async_copy(index_hbm, index_ref, sems.at[2]),
    ]
    for copy in copies:
        copy.start()
    for copy in copies:
        copy.wait()
    lane = lax.broadcasted_iota(jnp.int32, (3, 128), 1)
    picked = jnp.zeros((3, 128), F32)
    for slot in range(slots):
        star = index_ref[slot]
        tile = pl.ds(pl.multiple_of((star >> 7) << 7, 128), 128)
        shift = slot - star
        moved = pltpu.roll(pos_ref[:, tile], shift & 127, 1)
        picked = jnp.where(lane == slot, moved, picked)
        moved = pltpu.roll(vel_ref[:, tile], (shift + slots) & 127, 1)
        picked = jnp.where(lane == slot + slots, moved, picked)
    row = lax.broadcasted_iota(jnp.int32, (3, 128), 0)
    count = count_ref[...]
    mark = (row == 0) & (lane == slots - 1) & (count < slots)
    picked = jnp.where(mark, MARK + count.astype(F32), picked)

    def fill(part, carry):
        for k in range(3):
            send_ref[part, :, 128 * k : 128 * k + 128] = picked[k : k + 1]
        return carry

    lax.fori_loop(0, parts, fill, 0, unroll=8)


def pair_kernel(slots, recv_ref, pos_ref, vel_ref, mass_ref, send_ref, count_smem, offset_smem, dot_ref, sum_ref, slot_ref, own_ref, pull_ref, res_ref, sem):
    parts = recv_ref.shape[0]
    width = pos_ref.shape[1]
    copy = pltpu.make_async_copy(recv_ref.at[:, 0, 0:128], count_smem, sem)
    copy.start()

    def star_step(step, carry):
        cols = pl.ds(pl.multiple_of(step * 512, 512), 512)
        pos, vel, mass = pos_ref[:, cols], vel_ref[:, cols], mass_ref[:, cols]
        heavy = 3.0 * mass
        cross = jnp.sum(pos * vel, axis=0, keepdims=True)
        dots = pieces(jnp.concatenate([-heavy * vel, heavy, -heavy * pos, heavy * cross], axis=0))
        for k, (mine, _) in enumerate(PAIRS):
            dot_ref[8 * k : 8 * k + 8, cols] = dots[mine].astype(BF16)
        dot_ref[RAW:DEPTH, cols] = jnp.zeros((DEPTH - RAW, 512), BF16)
        sums = pieces(jnp.concatenate([mass * pos, mass, mass * vel, jnp.zeros_like(mass)], axis=0))
        for k in range(3):
            sum_ref[8 * k : 8 * k + 8, cols] = sums[k].astype(BF16)
        return carry

    lax.fori_loop(0, width // 512, star_step, 0, unroll=4)
    copy.wait()

    lane = lax.broadcasted_iota(jnp.int32, (8, 128), 1)
    row = lax.broadcasted_iota(jnp.int32, (8, 128), 0)

    def gather(part, total):
        offset_smem[part] = total
        raw = [recv_ref[part, :, 128 * k : 128 * k + 128] for k in range(3)]
        raw = jnp.concatenate([*raw, raw[0]], axis=0)
        own = jnp.concatenate([raw, pltpu.roll(raw, 128 - slots, 1)], axis=0)
        tile, start = total >> 7, total & 127
        moved = pltpu.roll(own, start, 1)
        slot_ref[tile] = jnp.where(lane < start, slot_ref[tile], moved)
        slot_ref[tile + 1] = moved
        last = count_smem[part, slots - 1]
        return total + jnp.where(last < MARK, slots, (last - MARK).astype(jnp.int32))

    total = lax.fori_loop(0, parts, gather, 0, unroll=32)

    def tile_step(tile, carry):
        slot = slot_ref[tile]
        cross = jnp.sum(slot[0:3] * slot[4:7], axis=0, keepdims=True)
        slot = jnp.where(row == 7, 1.0, jnp.where(row == 3, cross, slot))
        split = pieces(slot)
        rows = [split[theirs] for _, theirs in PAIRS] + [slot, jnp.zeros((DEPTH - RAW - 8, TILE), F32)]
        act = jnp.concatenate(rows, axis=0).T
        for k in range(3):
            own_ref[k] = jnp.broadcast_to(act[:, RAW + k : RAW + k + 1], (TILE, 128))
            pull_ref[k] = jnp.zeros((TILE, 128), F32)
        left = act.astype(BF16)

        def block_step(step, sums):
            for block in range(UNROLL):
                cols = pl.ds(pl.multiple_of((step * UNROLL + block) * BLOCK, BLOCK), BLOCK)
                dot = lax.dot_general(left, dot_ref[:, cols], NN, preferred_element_type=F32)
                high, low = [], []
                for chunk in range(TILE // CH):
                    part = slice(chunk * CH, chunk * CH + CH)
                    own = [own_ref[k, part, :] for k in range(3)]
                    acc = [pull_ref[k, part, :] for k in range(3)]
                    highs, lows = [], []
                    for half in range(BLOCK // 128):
                        lanes = pl.ds(pl.multiple_of((step * UNROLL + block) * BLOCK + half * 128, 128), 128)
                        star = [jnp.broadcast_to(pos_ref[k : k + 1, lanes], (CH, 128)) for k in range(3)]
                        dx = [star[k] - own[k] for k in range(3)]
                        squared = dx[2] * dx[2] + (dx[1] * dx[1] + (dx[0] * dx[0] + SOFTEN))
                        root = lax.rsqrt(squared)
                        inverse = root * root
                        cube = root * inverse
                        pull = (dot[part, half * 128 : half * 128 + 128] * inverse) * cube
                        for k in range(3):
                            acc[k] += pull * dx[k]
                        first = cube.astype(BF16)
                        highs.append(first)
                        lows.append((cube - first.astype(F32)).astype(BF16))
                    for k in range(3):
                        pull_ref[k, part, :] = acc[k]
                    high.append(jnp.concatenate(highs, axis=1))
                    low.append(jnp.concatenate(lows, axis=1))
                field = sum_ref[:, cols]
                sums += lax.dot_general(field, jnp.concatenate(high + low, axis=0), NT, preferred_element_type=F32)
            return sums

        sums = lax.fori_loop(0, width // (BLOCK * UNROLL), block_step, jnp.zeros((24, 2 * TILE), F32))
        sums = sums[:, :TILE] + sums[:, TILE:]
        sums = sums[0:8] + sums[8:16] + sums[16:24]
        pulls = [jnp.sum(pull_ref[k].T, axis=0, keepdims=True) for k in range(3)]
        pulls = jnp.concatenate([jnp.zeros((4, TILE), F32), *pulls, jnp.zeros((1, TILE), F32)], axis=0)
        res_ref[tile] = sums - slot * sums[3:4] - pulls
        return carry

    lax.fori_loop(0, (total + TILE - 1) // TILE, tile_step, 0)

    def spread(part, carry):
        first = offset_smem[part]
        tile, start = first >> 7, first & 127
        back = (128 - start) & 127
        moved = jnp.where(lane < 128 - start, pltpu.roll(res_ref[tile], back, 1), pltpu.roll(res_ref[tile + 1], back, 1))
        moved = jnp.where(lane[0:4] < slots, moved[0:4], pltpu.roll(moved[4:8], slots, 1))
        for k in range(3):
            send_ref[part, :, 128 * k : 128 * k + 128] = moved[k : k + 1]
        return carry

    lax.fori_loop(0, parts, spread, 0, unroll=32)


def finish_kernel(count_ref, recv_ref, accel_ref, jerk_ref):
    slots = accel_ref.shape[1]
    total = jnp.sum(recv_ref[...], axis=0)
    for k in range(3):
        row = total[:, 128 * k : 128 * k + 128]
        lane = lax.broadcasted_iota(jnp.int32, row.shape, 1)
        row = jnp.where(lane % slots < count_ref[...], row, 0.0)
        accel_ref[k : k + 1, :] = row[:, :slots]
        jerk_ref[k : k + 1, :] = row[:, slots : 2 * slots]


def pair_call(parts, slots, width):
    tiles = (parts * slots) // TILE + 2
    return pl.pallas_call(
        functools.partial(pair_kernel, slots),
        out_shape=jax.ShapeDtypeStruct((parts, 1, 384), F32),
        in_specs=[vmem()] * 4,
        out_specs=vmem(),
        scratch_shapes=[
            pltpu.SMEM((parts, 128), F32),
            pltpu.SMEM((parts,), jnp.int32),
            pltpu.VMEM((DEPTH, width), BF16),
            pltpu.VMEM((24, width), BF16),
            pltpu.VMEM((tiles, 8, 128), F32),
            pltpu.VMEM((3, TILE, 128), F32),
            pltpu.VMEM((3, TILE, 128), F32),
            pltpu.VMEM((tiles, 8, 128), F32),
            pltpu.SemaphoreType.DMA,
        ],
        compiler_params=pltpu.CompilerParams(vmem_limit_bytes=48 * 1024 * 1024),
    )


def body(parts, positions, velocities, masses, active_index, active_count):
    slots = active_index.shape[0]
    width = positions.shape[1]
    send = pl.pallas_call(
        functools.partial(prepare_kernel, parts),
        out_shape=jax.ShapeDtypeStruct((parts, 1, 384), F32),
        in_specs=[hbm(), vmem(), hbm(), hbm()],
        out_specs=vmem(),
        scratch_shapes=[
            pltpu.SMEM((slots,), jnp.int32),
            pltpu.VMEM((3, width), F32),
            pltpu.VMEM((3, width), F32),
            pltpu.SemaphoreType.DMA((3,)),
        ],
        compiler_params=pltpu.CompilerParams(vmem_limit_bytes=16 * 1024 * 1024),
    )(
        pltpu.with_memory_space_constraint(active_index, pltpu.HBM),
        active_count.reshape(1, 1),
        pltpu.with_memory_space_constraint(positions, pltpu.HBM),
        pltpu.with_memory_space_constraint(velocities, pltpu.HBM),
    )
    received = lax.all_to_all(send, AXES, 0, 0, tiled=True)
    partial_sums = pair_call(parts, slots, width)(received, positions, velocities, masses.reshape(1, width))
    returned = lax.all_to_all(partial_sums, AXES, 0, 0, tiled=True)
    return pl.pallas_call(
        finish_kernel,
        out_shape=(
            jax.ShapeDtypeStruct((3, slots), F32),
            jax.ShapeDtypeStruct((3, slots), F32),
        ),
        in_specs=[vmem(), vmem()],
        out_specs=(vmem(), vmem()),
        compiler_params=pltpu.CompilerParams(vmem_limit_bytes=16 * 1024 * 1024),
    )(active_count.reshape(1, 1), returned)


def solution(mesh):
    parts = int(np.prod([mesh.shape[axis] for axis in AXES]))
    return jax.shard_map(
        functools.partial(body, parts),
        mesh=mesh,
        in_specs=(P(None, AXES), P(None, AXES), P(AXES), P(AXES), P(AXES)),
        out_specs=(P(None, AXES), P(None, AXES)),
        check_vma=False,
    )
```

```python
import functools

import jax
import jax.numpy as jnp
import numpy as np
from jax import lax
from jax.experimental import pallas as pl
from jax.experimental.pallas import tpu as pltpu
from jax.sharding import PartitionSpec as P

AXES = ("col", "row")
SOFTEN = 0.0001
MARK = 8.0
F32 = jnp.float32
BF16 = jnp.bfloat16
TILE = 128
HALF = 64
CH = 16
BLOCK = 256
PAIRS = ((0, 0), (1, 0), (0, 1), (1, 1), (2, 0), (0, 2))
RAW = 8 * len(PAIRS)
DEPTH = 64
NN = (((1,), (0,)), ((), ()))
NT = (((1,), (1,)), ((), ()))


def vmem():
    return pl.BlockSpec(memory_space=pltpu.VMEM)


def hbm():
    return pl.BlockSpec(memory_space=pltpu.HBM)


def pieces(value):
    first = value.astype(BF16).astype(F32)
    rest = value - first
    second = rest.astype(BF16).astype(F32)
    return first, second, (rest - second).astype(BF16).astype(F32)


def prepare_kernel(parts, index_hbm, count_ref, pos_hbm, vel_hbm, send_ref, index_ref, pos_ref, vel_ref, sems):
    slots = index_ref.shape[0]
    copies = [
        pltpu.make_async_copy(pos_hbm, pos_ref, sems.at[0]),
        pltpu.make_async_copy(vel_hbm, vel_ref, sems.at[1]),
        pltpu.make_async_copy(index_hbm, index_ref, sems.at[2]),
    ]
    for copy in copies:
        copy.start()
    for copy in copies:
        copy.wait()
    lane = lax.broadcasted_iota(jnp.int32, (3, 128), 1)
    picked = jnp.zeros((3, 128), F32)
    for slot in range(slots):
        star = index_ref[slot]
        tile = pl.ds(pl.multiple_of((star >> 7) << 7, 128), 128)
        shift = slot - star
        moved = pltpu.roll(pos_ref[:, tile], shift & 127, 1)
        picked = jnp.where(lane == slot, moved, picked)
        moved = pltpu.roll(vel_ref[:, tile], (shift + slots) & 127, 1)
        picked = jnp.where(lane == slot + slots, moved, picked)
    row = lax.broadcasted_iota(jnp.int32, (3, 128), 0)
    count = count_ref[...]
    mark = (row == 0) & (lane == slots - 1) & (count < slots)
    picked = jnp.where(mark, MARK + count.astype(F32), picked)

    def fill(part, carry):
        for k in range(3):
            send_ref[part, :, 128 * k : 128 * k + 128] = picked[k : k + 1]
        return carry

    lax.fori_loop(0, parts, fill, 0, unroll=8)


def pair_kernel(slots, recv_ref, pos_ref, vel_ref, mass_ref, send_ref, count_smem, offset_smem, dot_ref, sum_ref, slot_ref, own_ref, pull_ref, res_ref, sem):
    parts = recv_ref.shape[0]
    width = pos_ref.shape[1]
    copy = pltpu.make_async_copy(recv_ref.at[:, 0, 0:128], count_smem, sem)
    copy.start()

    def star_step(step, carry):
        cols = pl.ds(pl.multiple_of(step * 512, 512), 512)
        pos, vel, mass = pos_ref[:, cols], vel_ref[:, cols], mass_ref[:, cols]
        heavy = 3.0 * mass
        cross = jnp.sum(pos * vel, axis=0, keepdims=True)
        dots = pieces(jnp.concatenate([-heavy * vel, heavy, -heavy * pos, heavy * cross], axis=0))
        for k, (mine, _) in enumerate(PAIRS):
            dot_ref[8 * k : 8 * k + 8, cols] = dots[mine].astype(BF16)
        dot_ref[RAW:DEPTH, cols] = jnp.zeros((DEPTH - RAW, 512), BF16)
        sums = pieces(jnp.concatenate([mass * pos, mass, mass * vel, jnp.zeros_like(mass)], axis=0))
        for k in range(3):
            sum_ref[8 * k : 8 * k + 8, cols] = sums[k].astype(BF16)
        return carry

    lax.fori_loop(0, width // 512, star_step, 0, unroll=4)
    copy.wait()

    lane = lax.broadcasted_iota(jnp.int32, (8, 128), 1)
    row = lax.broadcasted_iota(jnp.int32, (8, 128), 0)

    def gather(part, total):
        offset_smem[part] = total
        raw = [recv_ref[part, :, 128 * k : 128 * k + 128] for k in range(3)]
        raw = jnp.concatenate([*raw, raw[0]], axis=0)
        own = jnp.concatenate([raw, pltpu.roll(raw, 128 - slots, 1)], axis=0)
        tile, start = total >> 7, total & 127
        moved = pltpu.roll(own, start, 1)
        slot_ref[tile] = jnp.where(lane < start, slot_ref[tile], moved)
        slot_ref[tile + 1] = moved
        last = count_smem[part, slots - 1]
        return total + jnp.where(last < MARK, slots, (last - MARK).astype(jnp.int32))

    total = lax.fori_loop(0, parts, gather, 0, unroll=32)

    def lay_out(tile, place, height):
        slot = slot_ref[tile]
        cross = jnp.sum(slot[0:3] * slot[4:7], axis=0, keepdims=True)
        slot = jnp.where(row == 7, 1.0, jnp.where(row == 3, cross, slot))
        split = pieces(slot)
        rows = [split[theirs] for _, theirs in PAIRS] + [slot, jnp.zeros((DEPTH - RAW - 8, TILE), F32)]
        act = jnp.concatenate(rows, axis=0).T[:height]
        for k in range(3):
            own_ref[place, k, :height, :] = jnp.broadcast_to(act[:, RAW + k : RAW + k + 1], (height, 128))
            pull_ref[place, k, :height, :] = jnp.zeros((height, 128), F32)
        return slot, act.astype(BF16)

    def add_pairs(place, height, left):
        sums = jnp.zeros((24, 2 * height), F32)
        for block in range(width // BLOCK):
            cols = slice(block * BLOCK, block * BLOCK + BLOCK)
            dot = lax.dot_general(left, dot_ref[:, cols], NN, preferred_element_type=F32)
            high, low = [], []
            for chunk in range(height // CH):
                part = slice(chunk * CH, chunk * CH + CH)
                own = [own_ref[place, k, part, :] for k in range(3)]
                acc = [pull_ref[place, k, part, :] for k in range(3)]
                highs, lows = [], []
                for half in range(BLOCK // 128):
                    lanes = slice(block * BLOCK + half * 128, block * BLOCK + half * 128 + 128)
                    star = [jnp.broadcast_to(pos_ref[k : k + 1, lanes], (CH, 128)) for k in range(3)]
                    dx = [star[k] - own[k] for k in range(3)]
                    squared = dx[2] * dx[2] + (dx[1] * dx[1] + (dx[0] * dx[0] + SOFTEN))
                    root = lax.rsqrt(squared)
                    inverse = root * root
                    cube = root * inverse
                    pull = (dot[part, half * 128 : half * 128 + 128] * inverse) * cube
                    for k in range(3):
                        acc[k] += pull * dx[k]
                    first = cube.astype(BF16)
                    highs.append(first)
                    lows.append((cube - first.astype(F32)).astype(BF16))
                for k in range(3):
                    pull_ref[place, k, part, :] = acc[k]
                high.append(jnp.concatenate(highs, axis=1))
                low.append(jnp.concatenate(lows, axis=1))
            sums += lax.dot_general(sum_ref[:, cols], jnp.concatenate(high + low, axis=0), NT, preferred_element_type=F32)
        return sums

    def add_up(tile, place, height, slot, sums):
        sums = sums[:, :height] + sums[:, height:]
        sums = sums[0:8] + sums[8:16] + sums[16:24]
        pulls = [jnp.sum(pull_ref[place, k, :height, :].T, axis=0, keepdims=True) for k in range(3)]
        pulls = jnp.concatenate([jnp.zeros((4, height), F32), *pulls, jnp.zeros((1, height), F32)], axis=0)
        res_ref[tile, :, :height] = sums - slot[:, :height] * sums[3:4] - pulls

    def run(first, heights):
        laid = [lay_out(first + place, place, height) for place, height in enumerate(heights)]
        sums = [add_pairs(place, height, laid[place][1]) for place, height in enumerate(heights)]
        for place, height in enumerate(heights):
            add_up(first + place, place, height, laid[place][0], sums[place])

    halves = (total + HALF - 1) // HALF

    def two_tiles(step, carry):
        run(2 * step, (TILE, TILE))
        return carry

    lax.fori_loop(0, halves >> 2, two_tiles, 0)
    after = (halves >> 2) * 2

    @pl.when((halves & 2) != 0)
    def _():
        run(after, (TILE,))

    @pl.when((halves & 1) != 0)
    def _():
        run(halves >> 1, (HALF,))

    def spread(part, carry):
        first = offset_smem[part]
        tile, start = first >> 7, first & 127
        back = (128 - start) & 127
        moved = jnp.where(lane < 128 - start, pltpu.roll(res_ref[tile], back, 1), pltpu.roll(res_ref[tile + 1], back, 1))
        moved = jnp.where(lane[0:4] < slots, moved[0:4], pltpu.roll(moved[4:8], slots, 1))
        for k in range(3):
            send_ref[part, :, 128 * k : 128 * k + 128] = moved[k : k + 1]
        return carry

    lax.fori_loop(0, parts, spread, 0, unroll=32)


def finish_kernel(count_ref, recv_ref, accel_ref, jerk_ref):
    slots = accel_ref.shape[1]
    total = jnp.sum(recv_ref[...], axis=0)
    for k in range(3):
        row = total[:, 128 * k : 128 * k + 128]
        lane = lax.broadcasted_iota(jnp.int32, row.shape, 1)
        row = jnp.where(lane % slots < count_ref[...], row, 0.0)
        accel_ref[k : k + 1, :] = row[:, :slots]
        jerk_ref[k : k + 1, :] = row[:, slots : 2 * slots]


def pair_call(parts, slots, width):
    tiles = (parts * slots) // TILE + 2
    return pl.pallas_call(
        functools.partial(pair_kernel, slots),
        out_shape=jax.ShapeDtypeStruct((parts, 1, 384), F32),
        in_specs=[vmem()] * 4,
        out_specs=vmem(),
        scratch_shapes=[
            pltpu.SMEM((parts, 128), F32),
            pltpu.SMEM((parts,), jnp.int32),
            pltpu.VMEM((DEPTH, width), BF16),
            pltpu.VMEM((24, width), BF16),
            pltpu.VMEM((tiles, 8, 128), F32),
            pltpu.VMEM((2, 3, TILE, 128), F32),
            pltpu.VMEM((2, 3, TILE, 128), F32),
            pltpu.VMEM((tiles, 8, 128), F32),
            pltpu.SemaphoreType.DMA,
        ],
        compiler_params=pltpu.CompilerParams(vmem_limit_bytes=48 * 1024 * 1024),
    )


def body(parts, positions, velocities, masses, active_index, active_count):
    slots = active_index.shape[0]
    width = positions.shape[1]
    send = pl.pallas_call(
        functools.partial(prepare_kernel, parts),
        out_shape=jax.ShapeDtypeStruct((parts, 1, 384), F32),
        in_specs=[hbm(), vmem(), hbm(), hbm()],
        out_specs=vmem(),
        scratch_shapes=[
            pltpu.SMEM((slots,), jnp.int32),
            pltpu.VMEM((3, width), F32),
            pltpu.VMEM((3, width), F32),
            pltpu.SemaphoreType.DMA((3,)),
        ],
        compiler_params=pltpu.CompilerParams(vmem_limit_bytes=16 * 1024 * 1024),
    )(
        pltpu.with_memory_space_constraint(active_index, pltpu.HBM),
        active_count.reshape(1, 1),
        pltpu.with_memory_space_constraint(positions, pltpu.HBM),
        pltpu.with_memory_space_constraint(velocities, pltpu.HBM),
    )
    received = lax.all_to_all(send, AXES, 0, 0, tiled=True)
    partial_sums = pair_call(parts, slots, width)(received, positions, velocities, masses.reshape(1, width))
    returned = lax.all_to_all(partial_sums, AXES, 0, 0, tiled=True)
    return pl.pallas_call(
        finish_kernel,
        out_shape=(
            jax.ShapeDtypeStruct((3, slots), F32),
            jax.ShapeDtypeStruct((3, slots), F32),
        ),
        in_specs=[vmem(), vmem()],
        out_specs=(vmem(), vmem()),
        compiler_params=pltpu.CompilerParams(vmem_limit_bytes=16 * 1024 * 1024),
    )(active_count.reshape(1, 1), returned)


def solution(mesh):
    parts = int(np.prod([mesh.shape[axis] for axis in AXES]))
    return jax.shard_map(
        functools.partial(body, parts),
        mesh=mesh,
        in_specs=(P(None, AXES), P(None, AXES), P(AXES), P(AXES), P(AXES)),
        out_specs=(P(None, AXES), P(None, AXES)),
        check_vma=False,
    )
```

```python
import functools

import jax
import jax.numpy as jnp
import numpy as np
from jax import lax
from jax.experimental import pallas as pl
from jax.experimental.pallas import tpu as pltpu
from jax.sharding import PartitionSpec as P

AXES = ("col", "row")
SOFTEN = 0.0001
MARK = 8.0
F32 = jnp.float32
BF16 = jnp.bfloat16
TILE = 128
HALF = 64
CH = 16
BLOCK = 256
PAIRS = ((0, 0), (1, 0), (0, 1), (1, 1), (2, 0), (0, 2))
RAW = 8 * len(PAIRS)
DEPTH = 64
NN = (((1,), (0,)), ((), ()))
NT = (((1,), (1,)), ((), ()))


def vmem():
    return pl.BlockSpec(memory_space=pltpu.VMEM)


def hbm():
    return pl.BlockSpec(memory_space=pltpu.HBM)


def pieces(value):
    first = value.astype(BF16).astype(F32)
    rest = value - first
    second = rest.astype(BF16).astype(F32)
    return first, second, (rest - second).astype(BF16).astype(F32)


def prepare_kernel(parts, index_hbm, count_ref, pos_hbm, vel_hbm, send_ref, index_ref, pos_ref, vel_ref, sems):
    slots = index_ref.shape[0]
    copies = [
        pltpu.make_async_copy(pos_hbm, pos_ref, sems.at[0]),
        pltpu.make_async_copy(vel_hbm, vel_ref, sems.at[1]),
        pltpu.make_async_copy(index_hbm, index_ref, sems.at[2]),
    ]
    for copy in copies:
        copy.start()
    for copy in copies:
        copy.wait()
    lane = lax.broadcasted_iota(jnp.int32, (3, 128), 1)
    picked = jnp.zeros((3, 128), F32)
    for slot in range(slots):
        star = index_ref[slot]
        tile = pl.ds(pl.multiple_of((star >> 7) << 7, 128), 128)
        shift = slot - star
        moved = pltpu.roll(pos_ref[:, tile], shift & 127, 1)
        picked = jnp.where(lane == slot, moved, picked)
        moved = pltpu.roll(vel_ref[:, tile], (shift + slots) & 127, 1)
        picked = jnp.where(lane == slot + slots, moved, picked)
    row = lax.broadcasted_iota(jnp.int32, (3, 128), 0)
    count = count_ref[...]
    mark = (row == 0) & (lane == slots - 1) & (count < slots)
    picked = jnp.where(mark, MARK + count.astype(F32), picked)

    def fill(part, carry):
        for k in range(3):
            send_ref[part, :, 128 * k : 128 * k + 128] = picked[k : k + 1]
        return carry

    lax.fori_loop(0, parts, fill, 0, unroll=8)


def pair_kernel(slots, recv_ref, pos_ref, vel_ref, mass_ref, send_ref, count_smem, offset_smem, dot_ref, sum_ref, slot_ref, own_ref, pull_ref, res_ref, sem):
    parts = recv_ref.shape[0]
    width = pos_ref.shape[1]
    copy = pltpu.make_async_copy(recv_ref.at[:, 0, 0:128], count_smem, sem)
    copy.start()

    def star_step(step, carry):
        cols = pl.ds(pl.multiple_of(step * 512, 512), 512)
        pos, vel, mass = pos_ref[:, cols], vel_ref[:, cols], mass_ref[:, cols]
        heavy = 3.0 * mass
        cross = jnp.sum(pos * vel, axis=0, keepdims=True)
        dots = pieces(jnp.concatenate([-heavy * vel, heavy, -heavy * pos, heavy * cross], axis=0))
        for k, (mine, _) in enumerate(PAIRS):
            dot_ref[8 * k : 8 * k + 8, cols] = dots[mine].astype(BF16)
        sums = pieces(jnp.concatenate([mass * pos, mass, mass * vel, jnp.zeros_like(mass)], axis=0))
        for k in range(3):
            sum_ref[8 * k : 8 * k + 8, cols] = sums[k].astype(BF16)
        return carry

    lax.fori_loop(0, width // 512, star_step, 0, unroll=8)
    copy.wait()

    lane = lax.broadcasted_iota(jnp.int32, (8, 128), 1)
    row = lax.broadcasted_iota(jnp.int32, (8, 128), 0)

    def gather(part, total):
        offset_smem[part] = total
        raw = [recv_ref[part, :, 128 * k : 128 * k + 128] for k in range(3)]
        raw = jnp.concatenate([*raw, raw[0]], axis=0)
        own = jnp.concatenate([raw, pltpu.roll(raw, 128 - slots, 1)], axis=0)
        tile, start = total >> 7, total & 127
        moved = pltpu.roll(own, start, 1)
        slot_ref[tile] = jnp.where(lane < start, slot_ref[tile], moved)
        slot_ref[tile + 1] = moved
        last = count_smem[part, slots - 1]
        return total + jnp.where(last < MARK, slots, (last - MARK).astype(jnp.int32))

    total = lax.fori_loop(0, parts, gather, 0, unroll=32)

    def lay_out(tile, place, height):
        slot = slot_ref[tile]
        cross = jnp.sum(slot[0:3] * slot[4:7], axis=0, keepdims=True)
        slot = jnp.where(row == 7, 1.0, jnp.where(row == 3, cross, slot))
        split = pieces(slot)
        rows = [split[theirs] for _, theirs in PAIRS] + [slot, jnp.zeros((DEPTH - RAW - 8, TILE), F32)]
        act = jnp.concatenate(rows, axis=0).T[:height]
        for k in range(3):
            own_ref[place, k, :height, :] = jnp.broadcast_to(act[:, RAW + k : RAW + k + 1], (height, 128))
            pull_ref[place, k, :height, :] = jnp.zeros((height, 128), F32)
        return slot, act[:, :RAW].astype(BF16)

    def add_pairs(place, height, left):
        sums = jnp.zeros((24, 2 * height), F32)
        for block in range(width // BLOCK):
            cols = slice(block * BLOCK, block * BLOCK + BLOCK)
            dot = lax.dot_general(left, dot_ref[:RAW, cols], NN, preferred_element_type=F32)
            high, low = [], []
            for chunk in range(height // CH):
                part = slice(chunk * CH, chunk * CH + CH)
                own = [own_ref[place, k, part, :] for k in range(3)]
                acc = [pull_ref[place, k, part, :] for k in range(3)]
                highs, lows = [], []
                for half in range(BLOCK // 128):
                    lanes = slice(block * BLOCK + half * 128, block * BLOCK + half * 128 + 128)
                    star = [jnp.broadcast_to(pos_ref[k : k + 1, lanes], (CH, 128)) for k in range(3)]
                    dx = [star[k] - own[k] for k in range(3)]
                    squared = dx[2] * dx[2] + (dx[1] * dx[1] + (dx[0] * dx[0] + SOFTEN))
                    root = lax.rsqrt(squared)
                    inverse = root * root
                    cube = root * inverse
                    pull = (dot[part, half * 128 : half * 128 + 128] * inverse) * cube
                    for k in range(3):
                        acc[k] += pull * dx[k]
                    first = cube.astype(BF16)
                    highs.append(first)
                    lows.append((cube - first.astype(F32)).astype(BF16))
                for k in range(3):
                    pull_ref[place, k, part, :] = acc[k]
                high.append(jnp.concatenate(highs, axis=1))
                low.append(jnp.concatenate(lows, axis=1))
            sums += lax.dot_general(sum_ref[:, cols], jnp.concatenate(high + low, axis=0), NT, preferred_element_type=F32)
        return sums

    def add_up(tile, place, height, slot, sums):
        sums = sums[:, :height] + sums[:, height:]
        sums = sums[0:8] + sums[8:16] + sums[16:24]
        pulls = [jnp.sum(pull_ref[place, k, :height, :].T, axis=0, keepdims=True) for k in range(3)]
        pulls = jnp.concatenate([jnp.zeros((4, height), F32), *pulls, jnp.zeros((1, height), F32)], axis=0)
        res_ref[tile, :, :height] = sums - slot[:, :height] * sums[3:4] - pulls

    def run(first, heights):
        laid = [lay_out(first + place, place, height) for place, height in enumerate(heights)]
        sums = [add_pairs(place, height, laid[place][1]) for place, height in enumerate(heights)]
        for place, height in enumerate(heights):
            add_up(first + place, place, height, laid[place][0], sums[place])

    halves = (total + HALF - 1) // HALF

    def two_tiles(step, carry):
        run(2 * step, (TILE, TILE))
        return carry

    lax.fori_loop(0, halves >> 2, two_tiles, 0)
    after = (halves >> 2) * 2

    @pl.when((halves & 2) != 0)
    def _():
        run(after, (TILE,))

    @pl.when((halves & 1) != 0)
    def _():
        run(halves >> 1, (HALF,))

    def spread(part, carry):
        first = offset_smem[part]
        tile, start = first >> 7, first & 127
        back = (128 - start) & 127
        moved = jnp.where(lane < 128 - start, pltpu.roll(res_ref[tile], back, 1), pltpu.roll(res_ref[tile + 1], back, 1))
        moved = jnp.where(lane[0:4] < slots, moved[0:4], pltpu.roll(moved[4:8], slots, 1))
        for k in range(3):
            send_ref[part, :, 128 * k : 128 * k + 128] = moved[k : k + 1]
        return carry

    lax.fori_loop(0, parts, spread, 0, unroll=32)


def finish_kernel(count_ref, recv_ref, accel_ref, jerk_ref):
    slots = accel_ref.shape[1]
    total = jnp.sum(recv_ref[...], axis=0)
    for k in range(3):
        row = total[:, 128 * k : 128 * k + 128]
        lane = lax.broadcasted_iota(jnp.int32, row.shape, 1)
        row = jnp.where(lane % slots < count_ref[...], row, 0.0)
        accel_ref[k : k + 1, :] = row[:, :slots]
        jerk_ref[k : k + 1, :] = row[:, slots : 2 * slots]


def pair_call(parts, slots, width):
    tiles = (parts * slots) // TILE + 2
    return pl.pallas_call(
        functools.partial(pair_kernel, slots),
        out_shape=jax.ShapeDtypeStruct((parts, 1, 384), F32),
        in_specs=[vmem()] * 4,
        out_specs=vmem(),
        scratch_shapes=[
            pltpu.SMEM((parts, 128), F32),
            pltpu.SMEM((parts,), jnp.int32),
            pltpu.VMEM((RAW, width), BF16),
            pltpu.VMEM((24, width), BF16),
            pltpu.VMEM((tiles, 8, 128), F32),
            pltpu.VMEM((2, 3, TILE, 128), F32),
            pltpu.VMEM((2, 3, TILE, 128), F32),
            pltpu.VMEM((tiles, 8, 128), F32),
            pltpu.SemaphoreType.DMA,
        ],
        compiler_params=pltpu.CompilerParams(vmem_limit_bytes=48 * 1024 * 1024),
    )


def body(parts, positions, velocities, masses, active_index, active_count):
    slots = active_index.shape[0]
    width = positions.shape[1]
    send = pl.pallas_call(
        functools.partial(prepare_kernel, parts),
        out_shape=jax.ShapeDtypeStruct((parts, 1, 384), F32),
        in_specs=[hbm(), vmem(), hbm(), hbm()],
        out_specs=vmem(),
        scratch_shapes=[
            pltpu.SMEM((slots,), jnp.int32),
            pltpu.VMEM((3, width), F32),
            pltpu.VMEM((3, width), F32),
            pltpu.SemaphoreType.DMA((3,)),
        ],
        compiler_params=pltpu.CompilerParams(vmem_limit_bytes=16 * 1024 * 1024),
    )(
        pltpu.with_memory_space_constraint(active_index, pltpu.HBM),
        active_count.reshape(1, 1),
        pltpu.with_memory_space_constraint(positions, pltpu.HBM),
        pltpu.with_memory_space_constraint(velocities, pltpu.HBM),
    )
    received = lax.all_to_all(send, AXES, 0, 0, tiled=True)
    partial_sums = pair_call(parts, slots, width)(received, positions, velocities, masses.reshape(1, width))
    returned = lax.all_to_all(partial_sums, AXES, 0, 0, tiled=True)
    return pl.pallas_call(
        finish_kernel,
        out_shape=(
            jax.ShapeDtypeStruct((3, slots), F32),
            jax.ShapeDtypeStruct((3, slots), F32),
        ),
        in_specs=[vmem(), vmem()],
        out_specs=(vmem(), vmem()),
        compiler_params=pltpu.CompilerParams(vmem_limit_bytes=16 * 1024 * 1024),
    )(active_count.reshape(1, 1), returned)


def solution(mesh):
    parts = int(np.prod([mesh.shape[axis] for axis in AXES]))
    return jax.shard_map(
        functools.partial(body, parts),
        mesh=mesh,
        in_specs=(P(None, AXES), P(None, AXES), P(AXES), P(AXES), P(AXES)),
        out_specs=(P(None, AXES), P(None, AXES)),
        check_vma=False,
    )
```
